32 devices in a mesh: dp: 4 (over y, core), seq: 8 (over z, x).
Axes of the slice: x: 2, y: 2, z: 4, core: 2. Of those that a mesh axis runs over, the one named last changes fastest.
Arguments:
- tokens: bfloat16 [4, 2048, 2048], P('dp', 'seq'), may hold values from -6 to 6
- segment_ids: int32 [4, 2048], P('dp'), may hold values from 0 to 2, as said below
- ln1_gain: bfloat16 [2048], P('dp'), may hold values from 0.5 to 1.5
- ln1_bias: bfloat16 [2048], P('dp'), may hold values from -1.5 to 1.5
- w_qkv: bfloat16 [2048, 6144], P(('dp', 'seq')), may hold values from -0.1875 to 0.1875
- b_qkv: bfloat16 [6144], P('dp'), may hold values from -1.5 to 1.5
- w_out: bfloat16 [2048, 2048], P(('dp', 'seq')), may hold values from -0.375 to 0.375
- b_out: bfloat16 [2048], P('dp'), may hold values from -1.5 to 1.5
- ln2_gain: bfloat16 [2048], P('dp'), may hold values from 0.5 to 1.5
- ln2_bias: bfloat16 [2048], P('dp'), may hold values from -1.5 to 1.5
- w_up: bfloat16 [2048, 8192], P('dp', 'seq'), may hold values from -0.125 to 0.125
- b_up: bfloat16 [8192], P('seq'), may hold values from -1.5 to 1.5
- w_down: bfloat16 [8192, 2048], P('seq', 'dp'), may hold values from -0.09375 to 0.09375
- b_down: bfloat16 [2048], P('dp'), may hold values from -1.5 to 1.5
- cotangent: bfloat16 [4, 2048, 2048], P('dp', 'seq'), may hold values from -6 to 6
Outputs:
- layer_output: bfloat16 [4, 2048, 2048], P('dp', 'seq')
- input_grad: float32 [4, 2048, 2048], P('dp', 'seq')
- ln1_gain_grad: float32 [2048], replicated
- ln1_bias_grad: float32 [2048], replicated
- w_qkv_grad: float32 [2048, 6144], P(('dp', 'seq'))
- b_qkv_grad: float32 [6144], replicated
- w_out_grad: float32 [2048, 2048], P(('dp', 'seq'))
- b_out_grad: float32 [2048], replicated
- ln2_gain_grad: float32 [2048], replicated
- ln2_bias_grad: float32 [2048], replicated
- w_up_grad: float32 [2048, 8192], P('dp', 'seq')
- b_up_grad: float32 [8192], replicated
- w_down_grad: float32 [8192, 2048], P('seq', 'dp')
- b_down_grad: float32 [2048], replicated
- rms_stats: float32 [3], replicated
The draws below stay inside these ranges and needn't reach their ends.
Inputs may be any that keep to these rules, and one draw needn't show every extreme that they name: `segment_ids`: each row holds document 1 from position 0, then document 2, then a padding tail of id 0 that is never empty; ids never fall except into the padding.
All inputs are finite; a program needn't handle non-finite values.
Results may differ from the reference program's by a relative error of at most 0.02.
Values may be sent and summed in bfloat16 or wider, within the bound.
No kernel may reach another device: no remote copies, remote signals or barrier semaphores. Data moves between devices by JAX's collectives and lax.ppermute only.
A program may use at most 384 MiB of HBM per device.

```python
import jax
import jax.numpy as jnp
from jax import lax

D = 2048
HEADS = 16
FF = 8192
L = 2048
ROWS = 4


def draw_segment_ids(key, part):
    first_key, second_key = jax.random.split(key)
    first_len = jax.random.randint(first_key, (ROWS, 1), L // 4, 5 * L // 8 + 1)
    second_len = jax.random.randint(second_key, (ROWS, 1), L // 8, 5 * L // 16 + 1)
    places = jnp.arange(L, dtype=jnp.int32)[None, :]
    return jnp.where(places < first_len, 1, jnp.where(places < first_len + second_len, 2, 0)).astype(jnp.int32)


def steps_of(stream_key, shape, shards, smallest, largest):
    def one(position, shards_of):
        draws = jax.random.uniform(jax.random.fold_in(jax.random.fold_in(stream_key, 6), position), (shards_of,), jnp.float32, smallest / len(shards), largest / len(shards))
        return jnp.repeat(jnp.exp(draws), shape[position] // shards_of).reshape((-1,) + (1,) * (len(shape) - position - 1))

    level = one(*shards[0])
    for cut in shards[1:]:
        level = level * one(*cut)
    return level


def scatter_about(key, extent, width, most, cuts=(), kind=jnp.bfloat16):
    values = width * jax.random.normal(key, extent, jnp.float32)
    if cuts:
        values = values * steps_of(key, extent, cuts, -0.22, 0.18)
    return jnp.clip(values, -most, most).astype(kind)


def setup_inputs(seed: int = 0) -> dict:
    key_of = jax.random.split(jax.random.key(seed), 16)
    return {
        "tokens": scatter_about(key_of[0], (ROWS, L, D), 1.0, 6.0, ((0, 4), (1, 8))),
        "segment_ids": draw_segment_ids(jax.random.fold_in(key_of[15], 71), 0),
        "ln1_gain": jnp.clip(1.0 + 0.1 * jax.random.normal(key_of[2], (D,), jnp.float32), 0.5, 1.5).astype(jnp.bfloat16),
        "ln1_bias": scatter_about(key_of[3], (D,), 0.3, 1.5, ((0, 4),)),
        "w_qkv": scatter_about(key_of[4], (D, 3 * D), (D // 2) ** -0.5, 0.1875, ((0, 32),)),
        "b_qkv": scatter_about(key_of[5], (3 * D,), 0.3, 1.5, ((0, 4),)),
        "w_out": scatter_about(key_of[6], (D, D), (D // 8) ** -0.5, 0.375, ((0, 32),)),
        "b_out": scatter_about(key_of[7], (D,), 0.3, 1.5, ((0, 4),)),
        "ln2_gain": jnp.clip(1.0 + 0.1 * jax.random.normal(key_of[8], (D,), jnp.float32), 0.5, 1.5).astype(jnp.bfloat16),
        "ln2_bias": scatter_about(key_of[9], (D,), 0.3, 1.5, ((0, 4),)),
        "w_up": scatter_about(key_of[10], (D, FF), D ** -0.5, 0.125, ((0, 4), (1, 8))),
        "b_up": scatter_about(key_of[11], (FF,), 0.3, 1.5, ((0, 8),)),
        "w_down": scatter_about(key_of[12], (FF, D), (FF // 2) ** -0.5, 0.09375, ((0, 8), (1, 4))),
        "b_down": scatter_about(key_of[13], (D,), 0.3, 1.5, ((0, 4),)),
        "cotangent": scatter_about(key_of[14], (ROWS, L, D), 1.0, 6.0, ((0, 4), (1, 8))),
    }


EPSILON = 1e-05
NEG_FILL = -1e+30

@jax.custom_vjp
def low(v):
    return lax.optimization_barrier(v.astype(jnp.bfloat16)).astype(jnp.float32)

@jax.custom_vjp
def low_back(v):
    return v

def low_keep(v):
    return (low(v), None)

def low_pass(kept, grad):
    return (grad,)

def back_keep(v):
    return (v, None)

def back_low(kept, grad):
    return (low(grad),)
low.defvjp(low_keep, low_pass)
low_back.defvjp(back_keep, back_low)

def product(left, right):
    return jnp.dot(left, right, precision=lax.Precision.HIGHEST, preferred_element_type=jnp.float32)

def layer_norm(values, gain_vec, shift_vec):
    average = lax.optimization_barrier(jnp.mean(values, axis=-1, keepdims=True))
    centered = values - average
    variance = lax.optimization_barrier(jnp.mean(centered * centered, axis=-1, keepdims=True))
    return centered * lax.rsqrt(variance + EPSILON) * gain_vec + shift_vec

def positions_of(segments):
    length = segments.shape[-1]
    places = jnp.arange(length, dtype=jnp.int32)
    before = jnp.concatenate([jnp.full(segments.shape[:-1] + (1,), -1, jnp.int32), segments[..., :-1]], axis=-1)
    starts = lax.cummax(jnp.where(segments != before, places, 0), axis=segments.ndim - 1)
    return places - starts

def rotate(values, positions):
    half_size = values.shape[-1] // 2
    freqs_table = 10000.0 ** (-jnp.arange(half_size, dtype=jnp.float32) / half_size)
    angles = positions.astype(jnp.float32)[..., None, None] * freqs_table
    cosine = jnp.cos(angles)
    sine_part = jnp.sin(angles)
    first_half = values[..., :half_size]
    second_half = values[..., half_size:]
    return jnp.concatenate([first_half * cosine - second_half * sine_part, second_half * cosine + first_half * sine_part], axis=-1)

def row_forward(row_input, row_segments, params):
    gain_one, shift_one, qkv_weight, qkv_bias, out_weight, out_bias, gain_two, shift_two, up_weight, up_bias, down_weight, down_bias = params
    length, model_width = row_input.shape
    head_count = HEADS
    head_size = model_width // head_count
    split_shape = (length, head_count, head_size)
    places = positions_of(row_segments)
    normed_one = low(layer_norm(row_input, gain_one, shift_one))
    projected = low_back(product(normed_one, qkv_weight) + qkv_bias)
    queries = low(rotate(projected[:, :model_width].reshape(split_shape), places))
    keys_all = low(rotate(projected[:, model_width:2 * model_width].reshape(split_shape), places))
    values_all = low(projected[:, 2 * model_width:].reshape(split_shape))
    token_order = jnp.arange(length, dtype=jnp.int32)
    allowed = (row_segments[:, None] == row_segments[None, :]) & (token_order[None, :] <= token_order[:, None])
    score_scale = head_size ** (-0.5)

    def one_head(triple):
        query_head, key_head, value_head = triple
        scores = low_back(product(query_head, key_head.T) * score_scale)
        scores = jnp.where(allowed, scores, NEG_FILL)
        weights = low(jax.nn.softmax(scores, axis=-1))
        return product(weights, value_head)
    mixed_heads = lax.map(jax.checkpoint(one_head), (queries.transpose(1, 0, 2), keys_all.transpose(1, 0, 2), values_all.transpose(1, 0, 2)))
    attended = low_back(low(mixed_heads.transpose(1, 0, 2).reshape(length, model_width)))
    attn_branch = low_back(product(attended, out_weight) + out_bias)
    middle = row_input + attn_branch
    normed_two = low(layer_norm(middle, gain_two, shift_two))
    hidden_pre = low_back(product(normed_two, up_weight) + up_bias)
    activated = low(jax.nn.gelu(hidden_pre, approximate=True))
    mlp_branch = low_back(product(activated, down_weight) + down_bias)
    output = middle + mlp_branch
    valid_rows = (row_segments != 0)[:, None]
    square_sums = jnp.stack([jnp.sum(jnp.where(valid_rows, output * output, 0.0)), jnp.sum(jnp.where(valid_rows, attn_branch * attn_branch, 0.0)), jnp.sum(jnp.where(valid_rows, mlp_branch * mlp_branch, 0.0))])
    return (output, square_sums)

def reference(tokens, segment_ids, ln1_gain, ln1_bias, w_qkv, b_qkv, w_out, b_out, ln2_gain, ln2_bias, w_up, b_up, w_down, b_down, cotangent):
    params_in = (ln1_gain.astype(jnp.float32), ln1_bias.astype(jnp.float32), w_qkv.astype(jnp.float32), b_qkv.astype(jnp.float32), w_out.astype(jnp.float32), b_out.astype(jnp.float32), ln2_gain.astype(jnp.float32), ln2_bias.astype(jnp.float32), w_up.astype(jnp.float32), b_up.astype(jnp.float32), w_down.astype(jnp.float32), b_down.astype(jnp.float32))
    stream = tokens.astype(jnp.float32)

    def forward(stream_in, params):

        def row_step(running, row_item):
            row_input, row_segments = row_item
            row_output, row_sums = jax.checkpoint(row_forward)(row_input, row_segments, params)
            return (running + row_sums, row_output)
        totals, outputs = lax.scan(row_step, jnp.zeros((3,), jnp.float32), (stream_in, segment_ids))
        return (outputs, totals)
    outputs, pullback, totals = jax.vjp(forward, stream, params_in, has_aux=True)
    input_grad, grads = pullback(cotangent.astype(jnp.float32))
    counted = jnp.sum((segment_ids != 0).astype(jnp.float32))
    rms_stats = jnp.sqrt(totals / (counted * D))
    return (outputs.astype(jnp.bfloat16), input_grad, grads[0], grads[1], grads[2], grads[3], grads[4], grads[5], grads[6], grads[7], grads[8], grads[9], grads[10], grads[11], rms_stats)
```

```python
import functools

import jax
import jax.numpy as jnp
from jax import lax
from jax.experimental import pallas as pl
from jax.experimental.pallas import tpu as pltpu
from jax.sharding import Mesh
from jax.sharding import PartitionSpec as P

HEADS = 16
FF = 8192


EPSILON = 1e-05
NEG_FILL = -1e30


def layer_norm(values, gain_vec, shift_vec):
    average = jnp.mean(values, axis=-1, keepdims=True)
    centered = values - average
    variance = jnp.mean(centered * centered, axis=-1, keepdims=True)
    return centered * lax.rsqrt(variance + EPSILON) * gain_vec + shift_vec


def positions_of(segments):
    length = segments.shape[-1]
    places = jnp.arange(length, dtype=jnp.int32)
    before = jnp.concatenate(
        [jnp.full(segments.shape[:-1] + (1,), -1, jnp.int32), segments[..., :-1]], axis=-1
    )
    starts = lax.cummax(jnp.where(segments != before, places, 0), axis=segments.ndim - 1)
    return places - starts


def rotate(values, positions):
    half_size = values.shape[-1] // 2
    freqs_table = 10000.0 ** (-jnp.arange(half_size, dtype=jnp.float32) / half_size)
    angles = positions.astype(jnp.float32)[..., None, None] * freqs_table
    cosine = jnp.cos(angles)
    sine_part = jnp.sin(angles)
    first_half = values[..., :half_size]
    second_half = values[..., half_size:]
    return jnp.concatenate(
        [
            first_half * cosine - second_half * sine_part,
            second_half * cosine + first_half * sine_part,
        ],
        axis=-1,
    )


def rotate_back(gradient, positions):
    return jax.vjp(lambda inner_value: rotate(inner_value, positions), jnp.zeros_like(gradient))[1](
        gradient
    )[0]


def gelu_back(hidden_pre, act_grad):
    return jax.vjp(lambda inner_value: jax.nn.gelu(inner_value, approximate=True), hidden_pre)[1](
        act_grad
    )[0]


def score_block(query_row, key_row, allowed_row, score_scale):
    scores = (
        jnp.einsum("chd,khd->hck", query_row, key_row, preferred_element_type=jnp.float32)
        * score_scale
    )
    return jax.nn.softmax(jnp.where(allowed_row[None], scores, NEG_FILL), axis=-1)


def attend_rows(queries, keys_all, values_all, allowed, score_scale):

    def one_row(row_item):
        query_row, key_row, value_row, allowed_row = row_item
        weights = score_block(query_row, key_row, allowed_row, score_scale).astype(jnp.bfloat16)
        return jnp.einsum("hck,khd->chd", weights, value_row, preferred_element_type=jnp.float32)

    return lax.map(one_row, (queries, keys_all, values_all, allowed))


def attend_back(queries, keys_all, values_all, allowed, grad_heads, score_scale):

    def one_row(row_item):
        query_row, key_row, value_row, allowed_row, grad_row = row_item
        weights = score_block(query_row, key_row, allowed_row, score_scale)
        weight_grad = jnp.einsum(
            "chd,khd->hck", grad_row, value_row, preferred_element_type=jnp.float32
        )
        score_grad = weights * (
            weight_grad - jnp.sum(weights * weight_grad, axis=-1, keepdims=True)
        )
        score_low = score_grad.astype(jnp.bfloat16)
        query_grad = (
            jnp.einsum("hck,khd->chd", score_low, key_row, preferred_element_type=jnp.float32)
            * score_scale
        )
        key_grad = (
            jnp.einsum("hck,chd->khd", score_low, query_row, preferred_element_type=jnp.float32)
            * score_scale
        )
        value_grad = jnp.einsum(
            "hck,chd->khd",
            weights.astype(jnp.bfloat16),
            grad_row,
            preferred_element_type=jnp.float32,
        )
        return (query_grad, key_grad, value_grad)

    return lax.map(one_row, (queries, keys_all, values_all, allowed, grad_heads))


def local(
    tokens,
    segment_ids,
    ln1_gain,
    ln1_bias,
    w_qkv,
    b_qkv,
    w_out,
    b_out,
    ln2_gain,
    ln2_bias,
    w_up,
    b_up,
    w_down,
    b_down,
    cotangent,
):
    row_count, span_len, model_width = tokens.shape
    head_count = HEADS
    head_size = model_width // head_count
    score_scale = head_size ** (-0.5)
    seq_len = segment_ids.shape[1]
    split_shape = (row_count, span_len, head_count, head_size)
    flat_shape = (row_count, span_len, model_width)
    offset = lax.axis_index("seq") * span_len
    token_order = jnp.arange(seq_len, dtype=jnp.int32)
    local_order = offset + jnp.arange(span_len, dtype=jnp.int32)
    places = lax.dynamic_slice_in_dim(positions_of(segment_ids), offset, span_len, 1)
    local_segments = lax.dynamic_slice_in_dim(segment_ids, offset, span_len, 1)
    allowed = (local_segments[:, :, None] == segment_ids[:, None, :]) & (
        token_order[None, None, :] <= local_order[None, :, None]
    )
    stream = tokens.astype(jnp.float32)
    qkv_rows, out_rows = (
        lax.all_gather(w_qkv, "seq", axis=0, tiled=True),
        lax.all_gather(w_out, "seq", axis=0, tiled=True),
    )
    (
        qkv_weight,
        out_weight,
        up_slice,
        down_slice,
        gain_one,
        shift_one,
        qkv_bias,
        out_bias,
        gain_two,
        shift_two,
        down_bias,
    ) = (
        lax.all_gather(qkv_rows, "dp", axis=0, tiled=True),
        lax.all_gather(out_rows, "dp", axis=0, tiled=True),
        lax.all_gather(w_up, "dp", axis=0, tiled=True),
        lax.all_gather(w_down, "dp", axis=1, tiled=True),
        lax.all_gather(ln1_gain, "dp", axis=0, tiled=True),
        lax.all_gather(ln1_bias, "dp", axis=0, tiled=True),
        lax.all_gather(b_qkv, "dp", axis=0, tiled=True),
        lax.all_gather(b_out, "dp", axis=0, tiled=True),
        lax.all_gather(ln2_gain, "dp", axis=0, tiled=True),
        lax.all_gather(ln2_bias, "dp", axis=0, tiled=True),
        lax.all_gather(b_down, "dp", axis=0, tiled=True),
    )
    gain_one = gain_one.astype(jnp.float32)
    shift_one = shift_one.astype(jnp.float32)
    gain_two = gain_two.astype(jnp.float32)
    shift_two = shift_two.astype(jnp.float32)
    normed_one = layer_norm(stream, gain_one, shift_one).astype(jnp.bfloat16)
    projected = jnp.einsum(
        "rcd,de->rce", normed_one, qkv_weight, preferred_element_type=jnp.float32
    ) + qkv_bias.astype(jnp.float32)
    queries = rotate(projected[..., :model_width].reshape(split_shape), places).astype(jnp.bfloat16)
    keys_mine = rotate(
        projected[..., model_width : 2 * model_width].reshape(split_shape), places
    ).astype(jnp.bfloat16)
    values_mine = projected[..., 2 * model_width :].reshape(split_shape).astype(jnp.bfloat16)
    keys_all, values_all = (
        lax.all_gather(keys_mine, "seq", axis=1, tiled=True),
        lax.all_gather(values_mine, "seq", axis=1, tiled=True),
    )
    mixed_heads = attend_rows(queries, keys_all, values_all, allowed, score_scale)
    attended = mixed_heads.reshape(flat_shape).astype(jnp.bfloat16)
    attn_branch = jnp.einsum(
        "rcd,de->rce", attended, out_weight, preferred_element_type=jnp.float32
    ) + out_bias.astype(jnp.float32)
    middle = stream + attn_branch
    normed_two = layer_norm(middle, gain_two, shift_two).astype(jnp.bfloat16)
    normed_full = lax.all_gather(normed_two, "seq", axis=1, tiled=True)
    hidden_pre = jnp.einsum(
        "rld,df->rlf", normed_full, up_slice, preferred_element_type=jnp.float32
    ) + b_up.astype(jnp.float32)
    activated = jax.nn.gelu(hidden_pre, approximate=True).astype(jnp.bfloat16)
    partial_out = jnp.einsum(
        "rlf,fd->rld", activated, down_slice, preferred_element_type=jnp.float32
    )
    mlp_branch = lax.psum_scatter(
        partial_out.astype(jnp.bfloat16), "seq", scatter_dimension=1, tiled=True
    ).astype(jnp.float32) + down_bias.astype(jnp.float32)
    output = middle + mlp_branch
    valid_rows = (local_segments != 0)[..., None]
    square_sums = jnp.stack(
        [
            jnp.sum(jnp.where(valid_rows, output * output, 0.0)),
            jnp.sum(jnp.where(valid_rows, attn_branch * attn_branch, 0.0)),
            jnp.sum(jnp.where(valid_rows, mlp_branch * mlp_branch, 0.0)),
        ]
    )
    counted = jnp.sum((local_segments != 0).astype(jnp.float32))
    out_grad = cotangent.astype(jnp.float32)
    down_bias_grad = jnp.sum(out_grad, axis=(0, 1))
    low_full = lax.all_gather(cotangent, "seq", axis=1, tiled=True)
    down_weight_grad = jnp.einsum(
        "rlf,rld->fd", activated, low_full, preferred_element_type=jnp.float32
    )
    act_grad = jnp.einsum("rld,fd->rlf", low_full, down_slice, preferred_element_type=jnp.float32)
    up_low = gelu_back(hidden_pre, act_grad).astype(jnp.bfloat16)
    up_weight_grad = jnp.einsum(
        "rld,rlf->df", normed_full, up_low, preferred_element_type=jnp.float32
    )
    up_part = jnp.sum(up_low.astype(jnp.float32), axis=(0, 1))
    up_bias_grad = lax.dynamic_update_slice(
        jnp.zeros((FF,), jnp.float32), up_part, (lax.axis_index("seq") * up_part.shape[0],)
    )
    normed_terms = jnp.einsum("rlf,df->rld", up_low, up_slice, preferred_element_type=jnp.float32)
    normed_two_grad = lax.psum_scatter(
        normed_terms.astype(jnp.bfloat16), "seq", scatter_dimension=1, tiled=True
    ).astype(jnp.float32)
    up_grad_slice, down_grad_slice = (up_weight_grad, down_weight_grad)
    second_pull = jax.vjp(layer_norm, middle, gain_two, shift_two)[1]
    middle_part, gain_two_grad, shift_two_grad = second_pull(normed_two_grad)
    middle_grad = out_grad + middle_part
    attn_low = middle_grad.astype(jnp.bfloat16)
    out_weight_grad = jnp.einsum(
        "rcd,rce->de", attended, attn_low, preferred_element_type=jnp.float32
    )
    out_bias_grad = jnp.sum(attn_low.astype(jnp.float32), axis=(0, 1))
    attended_grad = jnp.einsum(
        "rce,de->rcd", attn_low, out_weight, preferred_element_type=jnp.float32
    )
    grad_heads = attended_grad.astype(jnp.bfloat16).reshape(split_shape)
    query_grad, key_grad_all, value_grad_all = attend_back(
        queries, keys_all, values_all, allowed, grad_heads, score_scale
    )
    key_grad, value_grad = (
        lax.psum_scatter(
            key_grad_all.astype(jnp.bfloat16), "seq", scatter_dimension=1, tiled=True
        ).astype(jnp.float32),
        lax.psum_scatter(
            value_grad_all.astype(jnp.bfloat16), "seq", scatter_dimension=1, tiled=True
        ).astype(jnp.float32),
    )
    projected_grad = jnp.concatenate(
        [
            rotate_back(query_grad, places).reshape(flat_shape),
            rotate_back(key_grad, places).reshape(flat_shape),
            value_grad.reshape(flat_shape),
        ],
        axis=-1,
    )
    projected_low = projected_grad.astype(jnp.bfloat16)
    qkv_weight_grad = jnp.einsum(
        "rcd,rce->de", normed_one, projected_low, preferred_element_type=jnp.float32
    )
    qkv_bias_grad = jnp.sum(projected_low.astype(jnp.float32), axis=(0, 1))
    normed_one_grad = jnp.einsum(
        "rce,de->rcd", projected_low, qkv_weight, preferred_element_type=jnp.float32
    )
    first_pull = jax.vjp(layer_norm, stream, gain_one, shift_one)[1]
    stream_part, gain_one_grad, shift_one_grad = first_pull(normed_one_grad)
    input_grad = middle_grad + stream_part
    qkv_grad_rows, out_grad_rows, up_grad_out, down_grad_out = (
        lax.psum_scatter(
            qkv_weight_grad.astype(jnp.bfloat16), "dp", scatter_dimension=0, tiled=True
        ).astype(jnp.float32),
        lax.psum_scatter(
            out_weight_grad.astype(jnp.bfloat16), "dp", scatter_dimension=0, tiled=True
        ).astype(jnp.float32),
        lax.psum_scatter(
            up_grad_slice.astype(jnp.bfloat16), "dp", scatter_dimension=0, tiled=True
        ).astype(jnp.float32),
        lax.psum_scatter(
            down_grad_slice.astype(jnp.bfloat16), "dp", scatter_dimension=1, tiled=True
        ).astype(jnp.float32),
    )
    qkv_grad_out, out_grad_out = (
        lax.psum_scatter(
            qkv_grad_rows.astype(jnp.bfloat16), "seq", scatter_dimension=0, tiled=True
        ).astype(jnp.float32),
        lax.psum_scatter(
            out_grad_rows.astype(jnp.bfloat16), "seq", scatter_dimension=0, tiled=True
        ).astype(jnp.float32),
    )
    (
        total_sums,
        total_count,
        gain_one_total,
        shift_one_total,
        qkv_bias_total,
        out_bias_total,
        gain_two_total,
        shift_two_total,
        up_bias_total,
        down_bias_total,
    ) = lax.psum(
        (
            square_sums,
            counted,
            gain_one_grad,
            shift_one_grad,
            qkv_bias_grad,
            out_bias_grad,
            gain_two_grad,
            shift_two_grad,
            up_bias_grad,
            down_bias_grad,
        ),
        ("dp", "seq"),
    )
    rms_stats = jnp.sqrt(total_sums / (total_count * model_width))
    return (
        output.astype(jnp.bfloat16),
        input_grad,
        gain_one_total,
        shift_one_total,
        qkv_grad_out,
        qkv_bias_total,
        out_grad_out,
        out_bias_total,
        gain_two_total,
        shift_two_total,
        up_grad_out,
        up_bias_total,
        down_grad_out,
        down_bias_total,
        rms_stats,
    )


PLANE_OF = (0, 3, 1, 2)
ROW_OF = (0, 2, 3, 1)
AXES = ("y", "core", "z", "x")
PLANE = ("y", "core", "x")
SWAP = [(0, 1), (1, 0)]
LOG2E = 1.4426950408889634


def trade(value, axis):
    return lax.ppermute(value, axis, SWAP)


def to_plane(value):
    pairs = []
    for r in range(4):
        for z in range(4):
            for x in range(2):
                pairs.append(((r * 4 + z) * 2 + x, (ROW_OF[z] * 4 + PLANE_OF[r]) * 2 + x))
    return lax.ppermute(value, AXES, pairs)


def gather_plane(block):
    half = block.shape[0] // 2
    from_x = trade(block, "x")
    from_y = trade(block, "y")
    top = trade(from_y[:half], "x")
    bottom = trade(from_x[half:], "y")
    return jnp.concatenate(
        [
            block,
            trade(block, "core"),
            from_y,
            trade(from_y, "core"),
            from_x,
            trade(from_x, "core"),
            top,
            bottom,
            trade(top, "core"),
            trade(bottom, "core"),
        ],
        axis=0,
    )


def scatter_plane(terms):
    f32 = jnp.float32
    span = terms.shape[0] // 8
    half = span // 2
    both = terms.reshape(2, 2, 2, span, -1)
    mate = trade(both[:, :, 1], "core")
    mine = (both[:, :, 0].astype(f32) + mate.astype(f32)).astype(jnp.bfloat16)
    across_x = trade(mine[1, 1, :half], "x")
    across_y = trade(mine[1, 1, half:], "y")
    x_top = trade(mine[1, 0, :half], "x")
    y_bottom = trade(mine[0, 1, half:], "y")
    y_top = trade((mine[0, 1, :half].astype(f32) + across_x.astype(f32)).astype(jnp.bfloat16), "y")
    x_bottom = trade((mine[1, 0, half:].astype(f32) + across_y.astype(f32)).astype(jnp.bfloat16), "x")
    own = mine[0, 0].astype(f32)
    return own + jnp.concatenate(
        [x_top.astype(f32) + y_top.astype(f32), x_bottom.astype(f32) + y_bottom.astype(f32)], axis=0
    )


def norm_parts(values):
    average = jnp.mean(values, axis=-1, keepdims=True)
    centered = values - average
    scale = lax.rsqrt(jnp.mean(centered * centered, axis=-1, keepdims=True) + EPSILON)
    return centered * scale, scale


def norm_back(unit, scale, gain_vec, grad):
    unit_grad = grad * gain_vec
    inner = unit_grad - jnp.mean(unit_grad, axis=-1, keepdims=True)
    inner = inner - unit * jnp.mean(unit_grad * unit, axis=-1, keepdims=True)
    return scale * inner, jnp.sum(grad * unit, axis=0), jnp.sum(grad, axis=0)


def turn(values, cosine, sine, sign):
    return values * cosine + sign * pltpu.roll(values, 64, 1) * sine


CONTRACT_LAST = (((1,), (1,)), ((), ()))
CONTRACT_FIRST = (((0,), (0,)), ((), ()))


def attend_kernel(slot_of, first_of, qkv_ref, begin_ref, out_ref, lse_ref, turned, *, tile, scale):
    i = pl.program_id(0)
    f32 = jnp.float32

    @pl.when(i == 0)
    def _():
        for h in range(2):
            whole = qkv_ref[:, 512 + 128 * h : 640 + 128 * h]
            turned[h] = whole.astype(f32).T.astype(jnp.bfloat16)

    begin = begin_ref[0]
    row = lax.broadcasted_iota(jnp.int32, (tile, tile), 0)
    col = lax.broadcasted_iota(jnp.int32, (tile, tile), 1)
    at = pl.multiple_of(slot_of[i] * tile, tile)
    queries = [qkv_ref[pl.ds(at, tile), 128 * h : 128 * h + 128] for h in range(2)]

    def scores(h, j, allowed):
        there = pl.multiple_of(slot_of[j] * tile, tile)
        keys = qkv_ref[pl.ds(there, tile), 256 + 128 * h : 384 + 128 * h]
        found = lax.dot_general(keys, queries[h], CONTRACT_LAST, preferred_element_type=f32) * scale
        return jnp.where(allowed, found, NEG_FILL), turned[h, :, pl.ds(there, tile)]

    state = []
    for h in range(2):
        found, values = scores(h, i, (row <= col) & (row + i * tile >= begin))
        top = jnp.max(found, axis=0, keepdims=True)
        weights = jnp.exp2(found - top)
        state.append(
            (
                top,
                jnp.sum(weights, axis=0, keepdims=True),
                jnp.dot(values, weights.astype(jnp.bfloat16), preferred_element_type=f32),
            )
        )

    def step(j, state):
        after = []
        allowed = row + j * tile >= begin
        for h in range(2):
            top, total, sums = state[h]
            found, values = scores(h, j, allowed)
            higher = jnp.maximum(top, jnp.max(found, axis=0, keepdims=True))
            shrink = jnp.exp2(top - higher)
            weights = jnp.exp2(found - higher)
            after.append(
                (
                    higher,
                    total * shrink + jnp.sum(weights, axis=0, keepdims=True),
                    sums * shrink
                    + jnp.dot(values, weights.astype(jnp.bfloat16), preferred_element_type=f32),
                )
            )
        return tuple(after)

    state = lax.fori_loop(first_of[i], i, step, tuple(state))
    for h in range(2):
        top, total, sums = state[h]
        out_ref[:, 128 * h : 128 * h + 128] = (sums / total).T.astype(jnp.bfloat16)
        lse_ref[0, h : h + 1, :] = top + jnp.log2(total)


def attend_back_kernel(
    slot_of,
    first_of,
    qkv_ref,
    begin_ref,
    lse_ref,
    out_ref,
    grad_ref,
    cos_ref,
    sin_ref,
    back_ref,
    key_sums,
    value_sums,
    *,
    tile,
    scale,
    plain,
):
    i = pl.program_id(0)
    f32 = jnp.float32

    @pl.when(i == 0)
    def _():
        key_sums[...] = jnp.zeros_like(key_sums)
        value_sums[...] = jnp.zeros_like(value_sums)

    begin = begin_ref[0]
    row = lax.broadcasted_iota(jnp.int32, (tile, tile), 0)
    col = lax.broadcasted_iota(jnp.int32, (tile, tile), 1)
    at = pl.multiple_of(slot_of[i] * tile, tile)
    queries = [qkv_ref[pl.ds(at, tile), 128 * h : 128 * h + 128] for h in range(2)]
    grads = [grad_ref[:, 128 * h : 128 * h + 128] for h in range(2)]
    inner = []
    for h in range(2):
        both = grads[h].astype(f32) * out_ref[:, 128 * h : 128 * h + 128].astype(f32)
        inner.append(jnp.sum(both.T, axis=0, keepdims=True))

    def pair(h, j, allowed, sums):
        there = pl.multiple_of(slot_of[j] * tile, tile)
        keys = qkv_ref[pl.ds(there, tile), 256 + 128 * h : 384 + 128 * h]
        values = qkv_ref[pl.ds(there, tile), 512 + 128 * h : 640 + 128 * h]
        found = lax.dot_general(keys, queries[h], CONTRACT_LAST, preferred_element_type=f32) * scale
        weights = jnp.where(allowed, jnp.exp2(found - lse_ref[0, h : h + 1, :]), 0.0)
        weight_grad = lax.dot_general(values, grads[h], CONTRACT_LAST, preferred_element_type=f32)
        score_low = (weights * (weight_grad - inner[h])).astype(jnp.bfloat16)
        value_sums[h, pl.ds(there, tile), :] += jnp.dot(
            weights.astype(jnp.bfloat16), grads[h], preferred_element_type=f32
        )
        key_sums[h, pl.ds(there, tile), :] += jnp.dot(
            score_low, queries[h], preferred_element_type=f32
        )
        return sums + lax.dot_general(score_low, keys, CONTRACT_FIRST, preferred_element_type=f32)

    state = []
    for h in range(2):
        state.append(
            pair(h, i, (row <= col) & (row + i * tile >= begin), jnp.zeros((tile, 128), f32))
        )

    def step(j, state):
        allowed = row + j * tile >= begin
        return tuple(pair(h, j, allowed, state[h]) for h in range(2))

    state = lax.fori_loop(first_of[i], i, step, tuple(state))
    cosine, sine = cos_ref[pl.ds(at, tile), :], sin_ref[pl.ds(at, tile), :]
    for h in range(2):
        back_ref[pl.ds(at, tile), 128 * h : 128 * h + 128] = (
            turn(state[h] * plain, cosine, sine, -1.0)
        ).astype(jnp.bfloat16)

    @pl.when(i == pl.num_programs(0) - 1)
    def _():
        for h in range(2):
            for s in range(8):
                rows = pl.ds(s * tile, tile)
                back_ref[rows, 256 + 128 * h : 384 + 128 * h] = turn(
                    key_sums[h, rows, :] * plain, cos_ref[rows, :], sin_ref[rows, :], -1.0
                ).astype(jnp.bfloat16)
                back_ref[rows, 512 + 128 * h : 640 + 128 * h] = value_sums[h, rows, :].astype(
                    jnp.bfloat16
                )


def attend(slot_of, first_of, qkv, begin):
    length = qkv.shape[0]
    tile = length // 8
    return pl.pallas_call(
        functools.partial(attend_kernel, tile=tile, scale=128**-0.5 * LOG2E),
        out_shape=(
            jax.ShapeDtypeStruct((length, 256), jnp.bfloat16),
            jax.ShapeDtypeStruct((8, 2, tile), jnp.float32),
        ),
        grid_spec=pltpu.PrefetchScalarGridSpec(
            num_scalar_prefetch=2,
            grid=(8,),
            in_specs=[
                pl.BlockSpec((length, 768), lambda i, s, f: (0, 0)),
                pl.BlockSpec((1, 1, tile), lambda i, s, f: (i, 0, 0)),
            ],
            out_specs=[
                pl.BlockSpec((tile, 256), lambda i, s, f: (s[i], 0)),
                pl.BlockSpec((1, 2, tile), lambda i, s, f: (i, 0, 0)),
            ],
            scratch_shapes=[pltpu.VMEM((2, 128, length), jnp.bfloat16)],
        ),
        compiler_params=pltpu.CompilerParams(vmem_limit_bytes=40 << 20),
        cost_estimate=pl.CostEstimate(flops=3 << 30, bytes_accessed=5 << 20, transcendentals=5 << 20),
        name="attend",
    )(slot_of, first_of, qkv, begin)


def attend_backward(slot_of, first_of, qkv, begin, lse, out, grad, cosine, sine):
    length = qkv.shape[0]
    tile = length // 8
    return pl.pallas_call(
        functools.partial(
            attend_back_kernel, tile=tile, scale=128**-0.5 * LOG2E, plain=128**-0.5
        ),
        out_shape=jax.ShapeDtypeStruct((length, 768), jnp.bfloat16),
        grid_spec=pltpu.PrefetchScalarGridSpec(
            num_scalar_prefetch=2,
            grid=(8,),
            in_specs=[
                pl.BlockSpec((length, 768), lambda i, s, f: (0, 0)),
                pl.BlockSpec((1, 1, tile), lambda i, s, f: (i, 0, 0)),
                pl.BlockSpec((1, 2, tile), lambda i, s, f: (i, 0, 0)),
                pl.BlockSpec((tile, 256), lambda i, s, f: (s[i], 0)),
                pl.BlockSpec((tile, 256), lambda i, s, f: (s[i], 0)),
                pl.BlockSpec((length, 128), lambda i, s, f: (0, 0)),
                pl.BlockSpec((length, 128), lambda i, s, f: (0, 0)),
            ],
            out_specs=pl.BlockSpec((length, 768), lambda i, s, f: (0, 0)),
            scratch_shapes=[
                pltpu.VMEM((2, length, 128), jnp.float32),
                pltpu.VMEM((2, length, 128), jnp.float32),
            ],
        ),
        compiler_params=pltpu.CompilerParams(vmem_limit_bytes=48 << 20),
        cost_estimate=pl.CostEstimate(flops=8 << 30, bytes_accessed=12 << 20, transcendentals=5 << 20),
        name="attend_back",
    )(slot_of, first_of, qkv, begin, lse, out, grad, cosine, sine)


def rotate_wide(values, cosine, sine):
    length = values.shape[0]
    heads = values.reshape(length, -1, 2, 64)
    swapped = heads[:, :, ::-1]
    turned = heads * cosine.reshape(length, 1, 2, 64) + swapped * sine.reshape(length, 1, 2, 64)
    return turned.reshape(length, -1)


def matmul(left, right, how="ab,bc->ac"):
    return jnp.einsum(how, left, right, preferred_element_type=jnp.float32)


def plane_local(
    tokens,
    segment_ids,
    ln1_gain,
    ln1_bias,
    w_qkv,
    b_qkv,
    w_out,
    b_out,
    ln2_gain,
    ln2_bias,
    w_up,
    b_up,
    w_down,
    b_down,
    cotangent,
):
    f32, bf16 = jnp.float32, jnp.bfloat16
    span, width = tokens.shape[1:]
    length = segment_ids.shape[1]
    my_y, my_core, my_z, my_x = (lax.axis_index(a) for a in AXES)
    my_r = my_y * 2 + my_core
    mine = my_r * 2 + my_x

    stream_low = to_plane(tokens[0])
    segments = to_plane(segment_ids)
    cot_low = to_plane(cotangent[0])

    piece = w_qkv.shape[0]
    part = w_qkv.reshape(piece, 3, 8, 256).transpose(2, 0, 1, 3).reshape(8 * piece, 768)
    part = lax.all_to_all(part, PLANE, 0, 0, tiled=True)
    qkv_all = lax.all_gather(part, "z", axis=0, tiled=True)
    qkv_weight = (
        qkv_all.reshape(4, 4, 2, piece, 768).transpose(1, 0, 2, 3, 4).reshape(width, 768)
    )
    out_all = lax.all_gather(w_out, "z", axis=0, tiled=False)
    low_half, high_half = out_all[:2], out_all[2:]
    keep = jnp.where(my_x == 0, low_half, high_half)
    give = jnp.where(my_x == 0, high_half, low_half)
    got = trade(give, "x")
    out_weight = jnp.stack(
        [jnp.where(my_x == 0, keep, got), jnp.where(my_x == 0, got, keep)], axis=1
    ).reshape(256, width)
    quarter = w_up.shape[1] // 4
    up_part = w_up.reshape(-1, 4, quarter).transpose(1, 0, 2)
    up_part = lax.all_to_all(up_part, ("y", "core"), 0, 0, tiled=True).reshape(width, quarter)
    up_weight = lax.all_gather(up_part, "z", axis=1, tiled=True)
    down_part = lax.all_to_all(
        w_down.reshape(4, quarter, -1), ("y", "core"), 0, 0, tiled=True
    )
    down_part = down_part.transpose(1, 0, 2).reshape(quarter, width)
    down_weight = lax.all_gather(down_part, "z", axis=0, tiled=True)

    small = jnp.concatenate([ln1_gain, ln1_bias, b_out, ln2_gain, ln2_bias, b_down, b_qkv, b_up])
    small = lax.all_gather(small, ("y", "core", "z"), axis=0, tiled=False)
    over_dp = small.reshape(4, 4, -1)[:, 0].astype(f32)
    step = ln1_gain.shape[0]
    gain_one, shift_one, out_bias, gain_two, shift_two, down_bias = (
        over_dp[:, k * step : (k + 1) * step].reshape(width) for k in range(6)
    )
    qkv_bias_all = over_dp[:, 6 * step : 9 * step].reshape(3, 8, 256)
    qkv_bias = lax.dynamic_index_in_dim(qkv_bias_all, mine, 1, keepdims=False).reshape(768)
    up_bias = lax.dynamic_slice_in_dim(
        small.reshape(4, 4, -1)[0, :, 9 * step :], my_r * quarter, quarter, 1
    )
    up_bias = up_bias.reshape(-1).astype(f32)

    plane_of = jnp.array(PLANE_OF, jnp.int32)
    slots = jnp.arange(8, dtype=jnp.int32)
    rows_of_slots = (my_y ^ ((slots >> 1) & 1)) * 2 + (my_core ^ (slots & 1))
    place_of = plane_of[rows_of_slots] * 2 + (my_x ^ (slots >> 2))
    slot_of = jnp.sum(
        jnp.where(place_of[None, :] == slots[:, None], slots[None, :], 0), axis=1
    ).astype(jnp.int32)
    places = positions_of(segments)[0]
    begin = (jnp.arange(length, dtype=jnp.int32) - places).reshape(8, 1, span)
    first_of = begin[:, 0, 0] // span
    by_slot = jnp.take(places.reshape(8, span), place_of, axis=0).reshape(length)
    freqs = 10000.0 ** (-jnp.arange(64, dtype=f32) / 64)
    angles = by_slot.astype(f32)[:, None] * freqs
    cos_half, sin_half = jnp.cos(angles), jnp.sin(angles)
    cosine = jnp.concatenate([cos_half, cos_half], axis=1)
    sine = jnp.concatenate([-sin_half, sin_half], axis=1)

    stream = stream_low.astype(f32)
    unit_one, scale_one = norm_parts(stream)
    normed_one = (unit_one * gain_one + shift_one).astype(bf16)
    normed_one_row = gather_plane(normed_one)
    projected = matmul(normed_one_row, qkv_weight) + qkv_bias
    qkv = jnp.concatenate(
        [rotate_wide(projected[:, :512], cosine, sine), projected[:, 512:]], axis=1
    ).astype(bf16)
    attended, lse = attend(slot_of, first_of, qkv, begin)
    attn_branch = scatter_plane(matmul(attended, out_weight).astype(bf16)) + out_bias
    middle = stream + attn_branch

    unit_two, scale_two = norm_parts(middle)
    normed_two = (unit_two * gain_two + shift_two).astype(bf16)
    normed_two_row = gather_plane(normed_two)
    hidden_pre = matmul(normed_two_row, up_weight) + up_bias
    activated = jax.nn.gelu(hidden_pre, approximate=True).astype(bf16)
    mlp_branch = scatter_plane(matmul(activated, down_weight).astype(bf16)) + down_bias
    output = middle + mlp_branch
    my_places = plane_of[my_r] * 2 + my_x
    valid = lax.dynamic_index_in_dim(segments.reshape(8, span), my_places, 0, keepdims=False) != 0
    valid_rows = valid[:, None]
    square_sums = jnp.stack(
        [
            jnp.sum(jnp.where(valid_rows, output * output, 0.0)),
            jnp.sum(jnp.where(valid_rows, attn_branch * attn_branch, 0.0)),
            jnp.sum(jnp.where(valid_rows, mlp_branch * mlp_branch, 0.0)),
            jnp.sum(valid.astype(f32)),
        ]
    )
    layer_output = to_plane(output.astype(bf16))

    cot_row = gather_plane(cot_low)
    out_grad = cot_low.astype(f32)
    down_bias_grad = jnp.sum(out_grad, axis=0)
    down_grad = matmul(activated, cot_row, "tf,td->fd")
    act_grad = matmul(cot_row, down_weight, "td,fd->tf")
    up_low = gelu_back(hidden_pre, act_grad).astype(bf16)
    up_grad = matmul(normed_two_row, up_low, "td,tf->df")
    up_bias_grad = jnp.sum(up_low.astype(f32), axis=0)
    normed_two_grad = scatter_plane(matmul(up_low, up_weight, "tf,df->td").astype(bf16))
    middle_part, gain_two_grad, shift_two_grad = norm_back(
        unit_two, scale_two, gain_two, normed_two_grad
    )
    middle_grad = out_grad + middle_part

    attn_low = middle_grad.astype(bf16)
    attn_low_row = gather_plane(attn_low)
    out_bias_grad = jnp.sum(attn_low.astype(f32), axis=0)
    attended_grad = matmul(attn_low_row, out_weight, "td,ed->te").astype(bf16)
    out_grad_part = matmul(attended, attn_low_row, "te,td->ed")
    projected_low = attend_backward(
        slot_of, first_of, qkv, begin, lse, attended, attended_grad, cosine, sine
    )
    qkv_grad = matmul(normed_one_row, projected_low, "td,te->de")
    qkv_bias_grad = jnp.sum(projected_low.astype(f32), axis=0)
    normed_one_grad = scatter_plane(matmul(projected_low, qkv_weight, "te,de->td").astype(bf16))
    stream_part, gain_one_grad, shift_one_grad = norm_back(
        unit_one, scale_one, gain_one, normed_one_grad
    )
    input_grad = to_plane((middle_grad + stream_part).astype(bf16)).astype(f32)

    def over_z(value):
        return lax.psum_scatter(value.astype(bf16), "z", scatter_dimension=0, tiled=True)

    down_out = over_z(down_grad).reshape(quarter, 4, -1).transpose(1, 0, 2)
    down_out = lax.all_to_all(down_out, ("y", "core"), 0, 0, tiled=True)
    down_out = down_out.reshape(4 * quarter, -1).astype(f32)
    up_out = over_z(up_grad.reshape(width, 4, quarter).transpose(1, 0, 2).reshape(-1, quarter))
    up_out = lax.all_to_all(up_out.reshape(4, -1, quarter), ("y", "core"), 0, 0, tiled=True)
    up_out = up_out.transpose(1, 0, 2).reshape(-1, 4 * quarter).astype(f32)
    out_parts = out_grad_part.astype(bf16).reshape(2, 2, -1, width)
    keep = jnp.where(my_x == 0, out_parts[:, 0], out_parts[:, 1])
    give = jnp.where(my_x == 0, out_parts[:, 1], out_parts[:, 0])
    got = trade(give, "x")
    out_parts = jnp.concatenate(
        [jnp.where(my_x == 0, keep, got), jnp.where(my_x == 0, got, keep)], axis=0
    )
    out_out = over_z(out_parts.reshape(-1, width)).astype(f32)
    qkv_parts = qkv_grad.astype(bf16).reshape(4, 4, 2, piece, 768).transpose(1, 0, 2, 3, 4)
    qkv_out = over_z(qkv_parts.reshape(width, 768))
    qkv_out = lax.all_to_all(qkv_out, PLANE, 0, 0, tiled=True)
    qkv_out = qkv_out.reshape(8, piece, 3, 256).transpose(1, 2, 0, 3).reshape(piece, -1).astype(f32)

    qkv_bias_terms = lax.dynamic_update_slice(
        jnp.zeros((3, 8, 256), f32), qkv_bias_grad.reshape(3, 1, 256), (0, mine, 0)
    )
    up_bias_terms = lax.dynamic_update_slice(
        jnp.zeros((4, 2, 4, quarter), f32),
        up_bias_grad.reshape(4, 1, 1, quarter),
        (0, my_x, my_r, 0),
    )
    (
        totals,
        gain_one_total,
        shift_one_total,
        qkv_bias_total,
        out_bias_total,
        gain_two_total,
        shift_two_total,
        up_bias_total,
        down_bias_total,
    ) = lax.psum(
        (
            square_sums,
            gain_one_grad,
            shift_one_grad,
            qkv_bias_terms.reshape(-1),
            out_bias_grad,
            gain_two_grad,
            shift_two_grad,
            up_bias_terms.reshape(-1),
            down_bias_grad,
        ),
        AXES,
    )
    rms_stats = jnp.sqrt(totals[:3] / (totals[3] * width))
    return (
        layer_output[None],
        input_grad[None],
        gain_one_total,
        shift_one_total,
        qkv_out,
        qkv_bias_total,
        out_out,
        out_bias_total,
        gain_two_total,
        shift_two_total,
        up_out,
        up_bias_total,
        down_out,
        down_bias_total,
        rms_stats,
    )


def plane_program(mesh):
    fine = Mesh(mesh.devices.reshape(2, 2, 4, 2), AXES)
    dp, seq, both = ("y", "core"), ("z", "x"), AXES
    return jax.shard_map(
        plane_local,
        mesh=fine,
        in_specs=(
            P(dp, seq, None),
            P(dp, None),
            P(dp),
            P(dp),
            P(both, None),
            P(dp),
            P(both, None),
            P(dp),
            P(dp),
            P(dp),
            P(dp, seq),
            P(seq),
            P(seq, dp),
            P(dp),
            P(dp, seq, None),
        ),
        out_specs=(
            P(dp, seq, None),
            P(dp, seq, None),
            P(),
            P(),
            P(both, None),
            P(),
            P(both, None),
            P(),
            P(),
            P(),
            P(dp, seq),
            P(),
            P(seq, dp),
            P(),
            P(),
        ),
        check_vma=False,
    )


def solution(mesh):
    if dict(mesh.shape) == {"dp": 4, "seq": 8}:
        return plane_program(mesh)
    placed = (
        P("dp", "seq", None),
        P("dp", None),
        P("dp"),
        P("dp"),
        P(("dp", "seq"), None),
        P("dp"),
        P(("dp", "seq"), None),
        P("dp"),
        P("dp"),
        P("dp"),
        P("dp", "seq"),
        P("seq"),
        P("seq", "dp"),
        P("dp"),
        P("dp", "seq", None),
    )
    return jax.shard_map(
        local,
        mesh=mesh,
        in_specs=placed,
        out_specs=(
            P("dp", "seq", None),
            P("dp", "seq", None),
            P(),
            P(),
            P(("dp", "seq"), None),
            P(),
            P(("dp", "seq"), None),
            P(),
            P(),
            P(),
            P("dp", "seq"),
            P(),
            P("seq", "dp"),
            P(),
            P(),
        ),
        check_vma=False,
    )
```
